32 devices in a mesh: leaf: 8 (over z, x), pair: 4 (over y, core).
Axes of the slice: x: 2, y: 2, z: 4, core: 2. Of those that a mesh axis runs over, the one named last changes fastest.
Arguments:
- points: float32 [64, 65536], P(None, ('pair', 'leaf')), may hold values from -6 to 6
- inv_scales: float32 [64], replicated, may hold values from 0.05 to 0.3
- direction: float32 [32, 65536], P(None, ('pair', 'leaf')), may hold values from -6 to 6
- residual: float32 [32, 65536], P(None, ('pair', 'leaf'))
- skeleton: int32 [32, 32], P(('pair', 'leaf')), may hold values from 0 to 2047, as said below
Outputs:
- product: float32 [32, 65536], P(None, ('pair', 'leaf'))
- dots: float32 [2, 32], replicated
The draws below stay inside these ranges and needn't reach their ends.
Inputs may be any that keep to these rules, and one draw needn't show every extreme that they name: `skeleton`: each row holds 32 distinct indices of points inside its own block of 2048, among them the block's first and last point.
All inputs are finite; a program needn't handle non-finite values.
Results may differ from the reference program's by a relative error of at most 0.0003.
Values sent between devices are 32-bit elements; how exact they have to be, the bound alone decides.
A program may use at most 64 MiB of HBM per device.

```python
import math
import jax
import jax.numpy as jnp
from jax import lax

F = 64
R = 32
SKEL = 32
LEAF_PTS = 2048
NBLOCKS = 32
NPTS = 65536
N_LEAF = 8
N_PAIR = 4


def draw_residual(key, part):
    key_base = jax.random.fold_in(key, 11)
    ramp = jnp.exp(math.log(3.0) * jnp.arange(NPTS, dtype=jnp.float32) / NPTS)
    values = jax.random.normal(key_base, (R, NPTS), jnp.float32) * ramp[None, :]
    return values.astype(jnp.float32)


def draw_skeleton(key, part):
    keys = jax.random.split(jax.random.fold_in(key, 21), NBLOCKS)
    inner = jax.vmap(lambda one_key: jax.random.permutation(one_key, LEAF_PTS - 2)[:SKEL - 2] + 1)(keys)
    first = jnp.zeros((NBLOCKS, 1), jnp.int32)
    last = jnp.full((NBLOCKS, 1), LEAF_PTS - 1, jnp.int32)
    picks = jnp.concatenate([first, inner.astype(jnp.int32), last], axis=1)
    return picks.astype(jnp.int32)


def levels(key, dims, cuts, low, top_value):
    def one(dim, parts):
        draws = jax.random.uniform(jax.random.fold_in(jax.random.fold_in(key, 6), dim), (parts,), jnp.float32, low / len(cuts), top_value / len(cuts))
        return jnp.repeat(jnp.exp(draws), dims[dim] // parts).reshape((-1,) + (1,) * (len(dims) - dim - 1))

    gain = one(*cuts[0])
    for cut in cuts[1:]:
        gain = gain * one(*cut)
    return gain


def scatter_about(own_key, dims, scale, bound, cuts=(), kind=jnp.bfloat16):
    array = scale * jax.random.normal(own_key, dims, jnp.float32)
    if cuts:
        array = array * levels(own_key, dims, cuts, -0.22, 0.18)
    return jnp.clip(array, -bound, bound).astype(kind)


def setup_inputs(seed: int = 0) -> dict:
    streams_of = jax.random.split(jax.random.key(seed), 6)
    points = scatter_about(streams_of[0], (F, NPTS), 1.0, 6.0, ((1, 32),), jnp.float32)
    inv_scales = jnp.clip(jnp.exp(jax.random.uniform(streams_of[1], (F,), jnp.float32, math.log(0.05), math.log(0.3))), 0.05, 0.3)
    direction = scatter_about(streams_of[2], (R, NPTS), 1.0, 6.0, ((1, 32),), jnp.float32)
    residual = draw_residual(jax.random.fold_in(streams_of[5], 71), 0)
    skeleton = draw_skeleton(jax.random.fold_in(streams_of[5], 71), 0)
    return {"points": points, "inv_scales": inv_scales, "direction": direction, "residual": residual, "skeleton": skeleton}


root_three = math.sqrt(3.0)
nugget = 0.5
far_weight = 0.125

def matern(left, right):
    norm_left = lax.optimization_barrier(jnp.sum(left * left, axis=0))
    norm_right = lax.optimization_barrier(jnp.sum(right * right, axis=0))
    cross = lax.dot_general(left, right, (((0,), (0,)), ((), ())), precision=lax.Precision.HIGHEST, preferred_element_type=jnp.float32)
    dist_sq = norm_left[:, None] + norm_right[None, :] - 2.0 * cross
    scaled_dist = root_three * jnp.sqrt(jnp.maximum(dist_sq, 0.0))
    return (1.0 + scaled_dist) * jnp.exp(-scaled_dist)

def matmul(left, right):
    return jnp.dot(left, right, precision=lax.Precision.HIGHEST, preferred_element_type=jnp.float32)

def reference(points, inv_scales, direction, residual, skeleton):
    nblk = N_LEAF * N_PAIR
    scaled = points * inv_scales[:, None]
    zblocks = jnp.transpose(scaled.reshape(F, nblk, LEAF_PTS), (1, 0, 2))
    vblocks = jnp.transpose(direction.reshape(R, nblk, LEAF_PTS), (1, 0, 2))
    position = jnp.arange(nblk) % N_LEAF
    has_left = (position > 0).astype(jnp.float32)
    has_right = (position < N_LEAF - 1).astype(jnp.float32)
    zero_z = jnp.zeros((1, F, LEAF_PTS), jnp.float32)
    zero_v = jnp.zeros((1, R, LEAF_PTS), jnp.float32)
    z_left = jnp.concatenate([zero_z, zblocks[:-1]], axis=0)
    z_right = jnp.concatenate([zblocks[1:], zero_z], axis=0)
    v_left = jnp.concatenate([zero_v, vblocks[:-1]], axis=0) * has_left[:, None, None]
    v_right = jnp.concatenate([vblocks[1:], zero_v], axis=0) * has_right[:, None, None]
    skel_pts = jnp.take_along_axis(zblocks, skeleton.astype(jnp.int32)[:, None, :], axis=2)

    def coeff_of(index):
        return matmul(vblocks[index], matern(zblocks[index], skel_pts[index]))
    coeffs = lax.map(coeff_of, jnp.arange(nblk))
    all_pts = jnp.transpose(skel_pts, (1, 0, 2)).reshape(F, nblk * SKEL)
    all_coeff = jnp.transpose(coeffs, (1, 0, 2)).reshape(R, nblk * SKEL)
    col_block = jnp.arange(nblk * SKEL) // SKEL
    amplitude = 1.0 / math.sqrt(3.0 * LEAF_PTS)

    def block_product(index):
        own_z = zblocks[index]
        cols_z = jnp.concatenate([z_left[index], own_z, z_right[index]], axis=1)
        cols_v = jnp.concatenate([v_left[index], vblocks[index], v_right[index]], axis=1)
        near = matmul(cols_v, matern(cols_z, own_z))
        far_mask = (col_block // N_LEAF != index // N_LEAF) | (jnp.abs(col_block % N_LEAF - index % N_LEAF) > 1)
        masked = all_coeff * far_mask.astype(jnp.float32)[None, :]
        own_pts = skel_pts[index]
        q_coeff = matmul(masked, matern(all_pts, own_pts))
        spread = matern(own_z, own_pts)
        far = lax.dot_general(q_coeff, spread, (((1,), (1,)), ((), ())), precision=lax.Precision.HIGHEST, preferred_element_type=jnp.float32)
        return nugget * vblocks[index] + amplitude * (near + far_weight * far)
    blocks_out = lax.map(block_product, jnp.arange(nblk))
    product = jnp.transpose(blocks_out, (1, 0, 2)).reshape(R, nblk * LEAF_PTS)
    total = nblk * LEAF_PTS
    squares = lax.optimization_barrier(jnp.sum(residual * residual, axis=1)) / total
    curvature = lax.optimization_barrier(jnp.sum(direction * product, axis=1)) / total
    return (product, jnp.stack([squares, curvature], axis=0))
```

```python
import functools
import math

import jax
import jax.numpy as jnp
from jax import lax
from jax.experimental import pallas as pl
from jax.experimental.pallas import tpu as pltpu
from jax.sharding import PartitionSpec as P

root_three = math.sqrt(3.0)
neg_log2e = -1.4426950408889634
nugget = 0.5
far_weight = 0.125
tiny = 1e-30
f32 = jnp.float32
bf16 = jnp.bfloat16
HI = lax.Precision.HIGHEST
TI = 256
TJ = 256
CH = 256


def matern_of(u):
    u = jnp.maximum(u, tiny)
    t = u * lax.rsqrt(u)
    return (1.0 + t) * jnp.exp2(t * neg_log2e)


def dot_nn(a, b):
    return lax.dot_general(a, b, (((1,), (0,)), ((), ())), precision=HI, preferred_element_type=f32)


def dot_nt(a, b):
    return lax.dot_general(a, b, (((1,), (1,)), ((), ())), precision=HI, preferred_element_type=f32)


def dot_tn(a, b):
    return lax.dot_general(a, b, (((0,), (0,)), ((), ())), precision=HI, preferred_element_type=f32)


def bdot(a, b):
    return jnp.dot(a, b, preferred_element_type=f32)


def split(x):
    h = x.astype(bf16)
    return h, (x - h.astype(f32)).astype(bf16)


def kernel(
    nleaf, npair, nblk_total,
    pts_ref, inv_ref, dir_ref, res_ref, skel_ref,
    prod_ref, dots_ref,
    halo_p, halo_d, b_ref, nb_ref, st_ref, ns_ref, dd_ref, acc_ref, ks_ref, ag_ref, red_a, red_b, tmp_ref,
    hs_sem, hr_sem, as_sem, ar_sem, bs_sem, br_sem, cs_sem, cr_sem, ds_sem, dr_sem,
):
    feats, n = pts_ref.shape
    rhs = dir_ref.shape[0]
    nskel = skel_ref.shape[1]
    leaf = lax.axis_index("leaf")
    pair = lax.axis_index("pair")

    def remote(src, dst, ss, rs, **dev):
        return pltpu.make_async_remote_copy(
            src_ref=src, dst_ref=dst, send_sem=ss, recv_sem=rs, device_id=dev,
            device_id_type=pl.DeviceIdType.MESH)

    def leaf_peer(k):
        return lax.rem(leaf + k, nleaf)

    def pair_peer(k):
        return lax.rem(pair + k, npair)

    barrier = pltpu.get_barrier_semaphore()
    for k in range(1, nleaf):
        pl.semaphore_signal(barrier, inc=1, device_id={"leaf": leaf_peer(k)}, device_id_type=pl.DeviceIdType.MESH)
    for k in range(1, npair):
        pl.semaphore_signal(barrier, inc=1, device_id={"pair": pair_peer(k)}, device_id_type=pl.DeviceIdType.MESH)
    pl.semaphore_wait(barrier, nleaf - 1 + npair - 1)

    has_left = leaf > 0
    has_right = leaf < nleaf - 1
    to_right = [
        remote(pts_ref, halo_p.at[0], hs_sem.at[0], hr_sem.at[0], leaf=leaf_peer(1)),
        remote(dir_ref, halo_d.at[0], hs_sem.at[1], hr_sem.at[1], leaf=leaf_peer(1)),
    ]
    to_left = [
        remote(pts_ref, halo_p.at[1], hs_sem.at[2], hr_sem.at[2], leaf=leaf_peer(nleaf - 1)),
        remote(dir_ref, halo_d.at[1], hs_sem.at[3], hr_sem.at[3], leaf=leaf_peer(nleaf - 1)),
    ]

    @pl.when(has_right)
    def _():
        for c in to_right:
            c.start()

    @pl.when(has_left)
    def _():
        for c in to_left:
            c.start()

    eye = lax.broadcasted_iota(jnp.int32, (feats, feats), 0) == lax.broadcasted_iota(jnp.int32, (feats, feats), 1)
    inv_col = jnp.sum(jnp.where(eye, jnp.broadcast_to(inv_ref[...], (feats, feats)), 0.0), axis=1, keepdims=True) * root_three

    def prep(p_src, d_src, own):
        @pl.loop(0, n // CH)
        def _(ci):
            cols = pl.ds(pl.multiple_of(ci * CH, CH), CH)
            p = p_src[:, cols] * inv_col
            h, l = split(p)
            hf, lf = h.astype(f32), l.astype(f32)
            q = hf + lf
            norm = jnp.sum(q * q, axis=0, keepdims=True)
            if own:
                b_ref[:, cols] = jnp.concatenate([h, l, h, l], axis=0)
                nb_ref[:, cols] = jnp.broadcast_to(norm, (8, CH))
            h2, l2 = hf * -2.0, lf * -2.0
            stack = jnp.concatenate([h2, h2, l2, l2], axis=0)
            st_ref[cols, :] = stack.T.astype(bf16)
            ns_ref[cols, :] = jnp.broadcast_to(norm, (128, CH)).T
            dh, dl = split(d_src[:, cols])
            dd_ref[:, cols] = jnp.concatenate([dh, dl], axis=0)

    def near_block(first):
        @pl.loop(0, n // TJ)
        def _(jt):
            cols = pl.ds(pl.multiple_of(jt * TJ, TJ), TJ)
            b = b_ref[:, cols]
            nb = nb_ref[0:1, cols]
            if first:
                a1 = jnp.zeros((2 * rhs, TJ), f32)
                a2 = jnp.zeros((rhs, TJ), f32)
            else:
                a1 = acc_ref[: 2 * rhs, cols]
                a2 = acc_ref[2 * rhs :, cols]
            for it in range(n // TI):
                rows = slice(it * TI, (it + 1) * TI)
                cross = bdot(st_ref[rows, :], b)
                nsr = ns_ref[rows, :]
                u = cross + jnp.concatenate([nsr] * (TJ // 128), axis=1) + nb
                k = matern_of(u)
                kh, kl = split(k)
                a1 = a1 + bdot(dd_ref[:, rows], kh)
                a2 = a2 + bdot(dd_ref[:rhs, rows], kl)
            acc_ref[: 2 * rhs, cols] = a1
            acc_ref[2 * rhs :, cols] = a2

    prep(pts_ref, dir_ref, True)

    onehot = (lax.broadcasted_iota(jnp.int32, (n, nskel), 0) == jnp.broadcast_to(skel_ref[...], (n, nskel)))
    onehot = jnp.where(onehot, 1.0, 0.0).astype(bf16)
    p_all = pts_ref[...] * inv_col
    s0 = p_all.astype(bf16)
    r1 = p_all - s0.astype(f32)
    s1 = r1.astype(bf16)
    s2 = (r1 - s1.astype(f32)).astype(bf16)
    skel_pts = bdot(s0, onehot) + bdot(s1, onehot) + bdot(s2, onehot)
    skel_rows = skel_pts.T
    norm_s = jnp.sum(skel_rows * skel_rows, axis=1, keepdims=True)
    norm_p = jnp.sum(p_all * p_all, axis=0, keepdims=True)
    ks = matern_of(norm_s + norm_p - 2.0 * dot_nn(skel_rows, p_all))
    ks_ref[...] = ks
    coeff_t = dot_nt(ks, dir_ref[...])
    pad = jnp.zeros((nskel, 128 - feats - rhs), f32)
    pack = jnp.concatenate([skel_rows, coeff_t, pad], axis=1)
    my_rows = pl.ds(pl.multiple_of(leaf * nskel, 8), nskel)
    ag_ref[pair, my_rows, :] = pack
    tmp_ref[...] = jnp.concatenate([skel_rows, jnp.zeros((nskel, 128 - feats), f32)], axis=1)

    stage_a = [
        remote(ag_ref.at[pair, my_rows, :], ag_ref.at[pair, my_rows, :], as_sem.at[k], ar_sem.at[k], leaf=leaf_peer(k))
        for k in range(1, nleaf)
    ]
    for c in stage_a:
        c.start()

    near_block(True)

    for k, c in enumerate(stage_a, 1):
        src_rows = pl.ds(pl.multiple_of(lax.rem(leaf + nleaf - k, nleaf) * nskel, 8), nskel)
        remote(ag_ref.at[pair, src_rows, :], ag_ref.at[pair, src_rows, :], as_sem.at[k], ar_sem.at[k], leaf=leaf_peer(k)).wait_recv()
    for c in stage_a:
        c.wait_send()
    stage_b = [
        remote(ag_ref.at[pair], ag_ref.at[pair], bs_sem.at[k], br_sem.at[k], pair=pair_peer(k))
        for k in range(1, npair)
    ]
    for c in stage_b:
        c.start()

    @pl.when(has_left)
    def _():
        for c in to_right:
            c.wait_recv()
        prep(halo_p.at[0], halo_d.at[0], False)
        near_block(False)

    for k, c in enumerate(stage_b, 1):
        src = lax.rem(pair + npair - k, npair)
        remote(ag_ref.at[src], ag_ref.at[src], bs_sem.at[k], br_sem.at[k], pair=pair_peer(k)).wait_recv()
    for c in stage_b:
        c.wait_send()

    width = nleaf * nskel
    own_rows = tmp_ref[...]
    own_norm = jnp.sum(own_rows * own_rows, axis=1, keepdims=True)
    is_pt = jnp.where(lax.broadcasted_iota(jnp.int32, (8, 128), 1) < feats, 1.0, 0.0)
    column_leaf = lax.div(lax.broadcasted_iota(jnp.int32, (nskel, width), 1), nskel)
    near_mask = jnp.abs(column_leaf - leaf) <= 1
    q_t = jnp.zeros((nskel, 128), f32)
    for p in range(npair):
        all_rows = ag_ref[p]
        cross = dot_nt(own_rows, all_rows)
        norm_all = dot_nt(is_pt, all_rows * all_rows)[0:1, :]
        w = matern_of(own_norm + norm_all - 2.0 * cross)
        same = jnp.full((nskel, width), pair, jnp.int32) == p
        w = jnp.where(jnp.logical_and(same, near_mask), 0.0, w)
        q_t = q_t + dot_nn(w, all_rows)
    q_t = q_t[:, feats : feats + rhs]
    prod_ref[...] = dot_tn(q_t, ks_ref[...])

    @pl.when(has_right)
    def _():
        for c in to_left:
            c.wait_recv()
        prep(halo_p.at[1], halo_d.at[1], False)
        near_block(False)

    amplitude = 1.0 / math.sqrt(3.0 * n)
    near = acc_ref[:rhs, :] + acc_ref[rhs : 2 * rhs, :] + acc_ref[2 * rhs :, :]
    direction = dir_ref[...]
    product = nugget * direction + amplitude * (near + far_weight * prod_ref[...])
    prod_ref[...] = product
    residual = res_ref[...]
    squares = jnp.sum(residual * residual, axis=1, keepdims=True)
    curvature = jnp.sum(direction * product, axis=1, keepdims=True)
    lane = lax.broadcasted_iota(jnp.int32, (rhs, 128), 1)
    both = jnp.where(lane == 0, squares, jnp.where(lane == 1, curvature, 0.0))
    both = jnp.concatenate([both, jnp.zeros((128 - rhs, 128), f32)], axis=0).T[0:8, :]
    red_a[leaf] = both
    sends = [
        remote(red_a.at[leaf], red_a.at[leaf], cs_sem.at[k], cr_sem.at[k], leaf=leaf_peer(k))
        for k in range(1, nleaf)
    ]
    for c in sends:
        c.start()
    for k in range(1, nleaf):
        src = lax.rem(leaf + nleaf - k, nleaf)
        remote(red_a.at[src], red_a.at[src], cs_sem.at[k], cr_sem.at[k], leaf=leaf_peer(k)).wait_recv()
    total = red_a[0]
    for k in range(1, nleaf):
        total = total + red_a[k]
    red_b[pair] = total
    sends_b = [
        remote(red_b.at[pair], red_b.at[pair], ds_sem.at[k], dr_sem.at[k], pair=pair_peer(k))
        for k in range(1, npair)
    ]
    for c in sends_b:
        c.start()
    for k in range(1, npair):
        src = lax.rem(pair + npair - k, npair)
        remote(red_b.at[src], red_b.at[src], ds_sem.at[k], dr_sem.at[k], pair=pair_peer(k)).wait_recv()
    total = red_b[0]
    for k in range(1, npair):
        total = total + red_b[k]
    dots_ref[...] = total[0:2, :rhs] * (1.0 / nblk_total)
    for c in sends + sends_b:
        c.wait_send()

    @pl.when(has_right)
    def _():
        for c in to_right:
            c.wait_send()

    @pl.when(has_left)
    def _():
        for c in to_left:
            c.wait_send()


def on_device(points, inv_scales, direction, residual, skeleton):
    feats, n = points.shape
    rhs = direction.shape[0]
    nskel = skeleton.shape[1]
    nleaf = lax.axis_size("leaf")
    npair = lax.axis_size("pair")
    vmem = pl.BlockSpec(memory_space=pltpu.VMEM)
    dma = pltpu.SemaphoreType.DMA
    return pl.pallas_call(
        functools.partial(kernel, nleaf, npair, n * nleaf * npair),
        out_shape=(jax.ShapeDtypeStruct((rhs, n), f32), jax.ShapeDtypeStruct((2, rhs), f32)),
        in_specs=[vmem] * 5,
        out_specs=(vmem, vmem),
        scratch_shapes=[
            pltpu.VMEM((2, feats, n), f32),
            pltpu.VMEM((2, rhs, n), f32),
            pltpu.VMEM((4 * feats, n), bf16),
            pltpu.VMEM((8, n), f32),
            pltpu.VMEM((n, 4 * feats), bf16),
            pltpu.VMEM((n, 128), f32),
            pltpu.VMEM((2 * rhs, n), bf16),
            pltpu.VMEM((3 * rhs, n), f32),
            pltpu.VMEM((nskel, n), f32),
            pltpu.VMEM((npair, nleaf * nskel, 128), f32),
            pltpu.VMEM((nleaf, 8, 128), f32),
            pltpu.VMEM((npair, 8, 128), f32),
            pltpu.VMEM((nskel, 128), f32),
            dma((4,)), dma((4,)),
            dma((nleaf,)), dma((nleaf,)),
            dma((npair,)), dma((npair,)),
            dma((nleaf,)), dma((nleaf,)),
            dma((npair,)), dma((npair,)),
        ],
        compiler_params=pltpu.CompilerParams(collective_id=0, has_side_effects=True, vmem_limit_bytes=60 * 1024 * 1024),
        name="matern_step",
    )(points, inv_scales.reshape(1, feats), direction, residual, skeleton)


def solution(mesh):
    return jax.shard_map(
        on_device,
        mesh=mesh,
        in_specs=(
            P(None, ("pair", "leaf")),
            P(),
            P(None, ("pair", "leaf")),
            P(None, ("pair", "leaf")),
            P(("pair", "leaf"), None),
        ),
        out_specs=(P(None, ("pair", "leaf")), P()),
        check_vma=False,
    )
```

```python
import functools
import math

import jax
import jax.numpy as jnp
from jax import lax
from jax.experimental import pallas as pl
from jax.experimental.pallas import tpu as pltpu
from jax.sharding import PartitionSpec as P

root_three = math.sqrt(3.0)
neg_log2e = -1.4426950408889634
nugget = 0.5
far_weight = 0.125
tiny = 1e-30
f32 = jnp.float32
bf16 = jnp.bfloat16
HI = lax.Precision.HIGHEST
TI = 256
CC = 512
FIRST = 2
CH = 256


def matern_of(u):
    u = jnp.maximum(u, tiny)
    t = u * lax.rsqrt(u)
    return (1.0 + t) * jnp.exp2(t * neg_log2e)


def dot_nn(a, b):
    return lax.dot_general(a, b, (((1,), (0,)), ((), ())), precision=HI, preferred_element_type=f32)


def dot_nt(a, b):
    return lax.dot_general(a, b, (((1,), (1,)), ((), ())), precision=HI, preferred_element_type=f32)


def dot_tn(a, b):
    return lax.dot_general(a, b, (((0,), (0,)), ((), ())), precision=HI, preferred_element_type=f32)


def bdot(a, b):
    return jnp.dot(a, b, preferred_element_type=f32)


def bdot_nt(a, b):
    return lax.dot_general(a, b, (((1,), (1,)), ((), ())), preferred_element_type=f32)


def split(x):
    h = x.astype(bf16)
    return h, (x - h.astype(f32)).astype(bf16)


def kernel(
    nleaf, npair, nblk_total,
    pts_ref, inv_ref, dir_ref, res_ref, skel_ref,
    prod_ref, dots_ref,
    halo_p, halo_d, ret_out, ret_in, b_ref, nb_ref, st_ref, ns_ref, dd_ref, acc_ref, ks_ref, ag_ref, red_a, red_b, tmp_ref,
    hs_sem, hr_sem, es_sem, er_sem, as_sem, ar_sem, bs_sem, br_sem, cs_sem, cr_sem, ds_sem, dr_sem,
):
    feats, n = pts_ref.shape
    rhs = dir_ref.shape[0]
    nskel = skel_ref.shape[1]
    leaf = lax.axis_index("leaf")
    pair = lax.axis_index("pair")

    def remote(src, dst, ss, rs, **dev):
        return pltpu.make_async_remote_copy(
            src_ref=src, dst_ref=dst, send_sem=ss, recv_sem=rs, device_id=dev,
            device_id_type=pl.DeviceIdType.MESH)

    def leaf_peer(k):
        return lax.rem(leaf + k, nleaf)

    def pair_peer(k):
        return lax.rem(pair + k, npair)

    barrier = pltpu.get_barrier_semaphore()
    for k in range(1, nleaf):
        pl.semaphore_signal(barrier, inc=1, device_id={"leaf": leaf_peer(k)}, device_id_type=pl.DeviceIdType.MESH)
    for k in range(1, npair):
        pl.semaphore_signal(barrier, inc=1, device_id={"pair": pair_peer(k)}, device_id_type=pl.DeviceIdType.MESH)
    pl.semaphore_wait(barrier, nleaf - 1 + npair - 1)

    has_left = leaf > 0
    has_right = leaf < nleaf - 1
    left = leaf_peer(nleaf - 1)
    right = leaf_peer(1)

    def chunk(ci):
        return pl.ds(pl.multiple_of(ci * CC, CC), CC)

    def halo(ci):
        cols = chunk(ci)
        return (
            remote(pts_ref.at[:, cols], halo_p.at[:, cols], hs_sem.at[0, ci], hr_sem.at[0, ci], leaf=left),
            remote(dir_ref.at[:, cols], halo_d.at[:, cols], hs_sem.at[1, ci], hr_sem.at[1, ci], leaf=left),
        )

    def give_back(ci):
        cols = chunk(ci)
        return remote(ret_out.at[:, cols], ret_in.at[:, cols], es_sem.at[ci], er_sem.at[ci], leaf=right)

    def send_halo(lo, hi):
        @pl.when(has_left)
        def _():
            for ci in range(lo, hi):
                for c in halo(ci):
                    c.start()

    send_halo(0, FIRST)

    eye = lax.broadcasted_iota(jnp.int32, (feats, feats), 0) == lax.broadcasted_iota(jnp.int32, (feats, feats), 1)
    inv_col = jnp.sum(jnp.where(eye, jnp.broadcast_to(inv_ref[...], (feats, feats)), 0.0), axis=1, keepdims=True) * root_three

    def halves(p_src, d_src, cols):
        p = p_src[:, cols] * inv_col
        h, l = split(p)
        hf, lf = h.astype(f32), l.astype(f32)
        q = hf + lf
        norm = jnp.sum(q * q, axis=0, keepdims=True)
        dh, dl = split(d_src[:, cols])
        return jnp.concatenate([h, l, h, l], axis=0), jnp.concatenate([dh, dl], axis=0), hf, lf, norm

    @pl.loop(0, n // CH)
    def _(ci):
        cols = pl.ds(pl.multiple_of(ci * CH, CH), CH)
        b, dd, hf, lf, norm = halves(pts_ref, dir_ref, cols)
        b_ref[:, cols] = b
        dd_ref[:, cols] = dd
        nb_ref[:, cols] = jnp.broadcast_to(norm, (8, CH))
        h2, l2 = hf * -2.0, lf * -2.0
        st_ref[cols, :] = jnp.concatenate([h2, h2, l2, l2], axis=0).T.astype(bf16)
        ns_ref[cols, :] = jnp.broadcast_to(norm, (128, CH)).T
        acc_ref[:, cols] = jnp.zeros((rhs, CH), f32)

    nt = n // TI

    def tiles(rows_of, count, b, nb):
        nxt = bdot(st_ref[rows_of(0), :], b)
        for i in range(count):
            cross = nxt
            if i + 1 < count:
                nxt = bdot(st_ref[rows_of(i + 1), :], b)
            u = cross + jnp.concatenate([ns_ref[rows_of(i), :]] * (b.shape[1] // 128), axis=1) + nb
            kh, kl = split(matern_of(u))
            yield i, kh, kl

    def own_block():
        @pl.loop(0, nt)
        def _(jt):
            cols = pl.ds(pl.multiple_of(jt * TI, TI), TI)
            b = b_ref[:, cols]
            nb = nb_ref[0:1, cols]
            ddj = dd_ref[:, cols]
            a1 = jnp.zeros((2 * rhs, TI), f32)
            a2 = jnp.zeros((rhs, TI), f32)

            def rows_of(d):
                return pl.ds(pl.multiple_of(lax.rem(jt + nt - d, nt) * TI, TI), TI)

            later = []
            for d, kh, kl in tiles(rows_of, nt // 2 + 1, b, nb):
                rows = rows_of(d)
                a1 = a1 + bdot(dd_ref[:, rows], kh)
                a2 = a2 + bdot(dd_ref[:rhs, rows], kl)
                if 0 < d and 2 * d < nt:
                    r1 = bdot_nt(ddj, kh)
                    later.append((rows, r1[:rhs] + r1[rhs:] + bdot_nt(ddj[:rhs], kl)))
            acc_ref[:, cols] += a1[:rhs] + a1[rhs:] + a2
            for rows, part in later:
                acc_ref[:, rows] += part

    def pair_chunk(ci):
        for c in halo(ci):
            c.wait_recv()

        @pl.loop(0, CC // TI)
        def _(half):
            cols = pl.ds(pl.multiple_of(ci * CC + half * TI, TI), TI)
            b, ddj, _, _, nb = halves(halo_p, halo_d, cols)
            a1 = jnp.zeros((2 * rhs, TI), f32)
            a2 = jnp.zeros((rhs, TI), f32)
            for it, kh, kl in tiles(lambda i: slice(i * TI, (i + 1) * TI), nt, b, nb):
                rows = slice(it * TI, (it + 1) * TI)
                a1 = a1 + bdot(dd_ref[:, rows], kh)
                a2 = a2 + bdot(dd_ref[:rhs, rows], kl)
                r1 = bdot_nt(ddj, kh)
                acc_ref[:, rows] += r1[:rhs] + r1[rhs:] + bdot_nt(ddj[:rhs], kl)
            ret_out[:, cols] = a1[:rhs] + a1[rhs:] + a2

        give_back(ci).start()

    onehot = (lax.broadcasted_iota(jnp.int32, (n, nskel), 0) == jnp.broadcast_to(skel_ref[...], (n, nskel)))
    onehot = jnp.where(onehot, 1.0, 0.0).astype(bf16)
    p_all = pts_ref[...] * inv_col
    s0 = p_all.astype(bf16)
    r1 = p_all - s0.astype(f32)
    s1 = r1.astype(bf16)
    s2 = (r1 - s1.astype(f32)).astype(bf16)
    skel_pts = bdot(s0, onehot) + bdot(s1, onehot) + bdot(s2, onehot)
    skel_rows = skel_pts.T
    norm_s = jnp.sum(skel_rows * skel_rows, axis=1, keepdims=True)
    norm_p = jnp.sum(p_all * p_all, axis=0, keepdims=True)
    ks = matern_of(norm_s + norm_p - 2.0 * dot_nn(skel_rows, p_all))
    ks_ref[...] = ks
    coeff_t = dot_nt(ks, dir_ref[...])
    pad = jnp.zeros((nskel, 128 - feats - rhs), f32)
    pack = jnp.concatenate([skel_rows, coeff_t, pad], axis=1)
    my_rows = pl.ds(pl.multiple_of(leaf * nskel, 8), nskel)
    ag_ref[pair, my_rows, :] = pack
    tmp_ref[...] = jnp.concatenate([skel_rows, jnp.zeros((nskel, 128 - feats), f32)], axis=1)

    stage_a = [
        remote(ag_ref.at[pair, my_rows, :], ag_ref.at[pair, my_rows, :], as_sem.at[k], ar_sem.at[k], leaf=leaf_peer(k))
        for k in range(1, nleaf)
    ]
    for c in stage_a:
        c.start()

    send_halo(FIRST, n // CC)
    own_block()

    stage_b = [
        remote(ag_ref.at[pair], ag_ref.at[pair], bs_sem.at[k], br_sem.at[k], pair=pair_peer(k))
        for k in range(1, npair)
    ]

    @pl.loop(0, n // CC)
    def _(ci):
        @pl.when(ci == n // CC - 1)
        def _():
            for k, c in enumerate(stage_a, 1):
                src_rows = pl.ds(pl.multiple_of(lax.rem(leaf + nleaf - k, nleaf) * nskel, 8), nskel)
                remote(ag_ref.at[pair, src_rows, :], ag_ref.at[pair, src_rows, :], as_sem.at[k], ar_sem.at[k], leaf=leaf_peer(k)).wait_recv()
            for c in stage_a:
                c.wait_send()
            for c in stage_b:
                c.start()

        @pl.when(has_right)
        def _():
            pair_chunk(ci)

    for k, c in enumerate(stage_b, 1):
        src = lax.rem(pair + npair - k, npair)
        remote(ag_ref.at[src], ag_ref.at[src], bs_sem.at[k], br_sem.at[k], pair=pair_peer(k)).wait_recv()
    for c in stage_b:
        c.wait_send()

    width = nleaf * nskel
    own_rows = tmp_ref[...]
    own_norm = jnp.sum(own_rows * own_rows, axis=1, keepdims=True)
    is_pt = jnp.where(lax.broadcasted_iota(jnp.int32, (8, 128), 1) < feats, 1.0, 0.0)
    column_leaf = lax.div(lax.broadcasted_iota(jnp.int32, (nskel, width), 1), nskel)
    near_mask = jnp.abs(column_leaf - leaf) <= 1
    q_t = jnp.zeros((nskel, 128), f32)
    for p in range(npair):
        all_rows = ag_ref[p]
        cross = dot_nt(own_rows, all_rows)
        norm_all = dot_nt(is_pt, all_rows * all_rows)[0:1, :]
        w = matern_of(own_norm + norm_all - 2.0 * cross)
        same = jnp.full((nskel, width), pair, jnp.int32) == p
        w = jnp.where(jnp.logical_and(same, near_mask), 0.0, w)
        q_t = q_t + dot_nn(w, all_rows)
    q_t = q_t[:, feats : feats + rhs]
    far = dot_tn(q_t, ks_ref[...])
    prod_ref[...] = far_weight * far + acc_ref[...]

    @pl.when(has_left)
    def _():
        for ci in range(n // CC):
            give_back(ci).wait_recv()
        prod_ref[...] += ret_in[...]

    amplitude = 1.0 / math.sqrt(3.0 * n)
    direction = dir_ref[...]
    product = nugget * direction + amplitude * prod_ref[...]
    prod_ref[...] = product
    residual = res_ref[...]
    squares = jnp.sum(residual * residual, axis=1, keepdims=True)
    curvature = jnp.sum(direction * product, axis=1, keepdims=True)
    lane = lax.broadcasted_iota(jnp.int32, (rhs, 128), 1)
    both = jnp.where(lane == 0, squares, jnp.where(lane == 1, curvature, 0.0))
    both = jnp.concatenate([both, jnp.zeros((128 - rhs, 128), f32)], axis=0).T[0:8, :]
    red_a[leaf] = both
    sends = [
        remote(red_a.at[leaf], red_a.at[leaf], cs_sem.at[k], cr_sem.at[k], leaf=leaf_peer(k))
        for k in range(1, nleaf)
    ]
    for c in sends:
        c.start()
    for k in range(1, nleaf):
        src = lax.rem(leaf + nleaf - k, nleaf)
        remote(red_a.at[src], red_a.at[src], cs_sem.at[k], cr_sem.at[k], leaf=leaf_peer(k)).wait_recv()
    total = red_a[0]
    for k in range(1, nleaf):
        total = total + red_a[k]
    red_b[pair] = total
    sends_b = [
        remote(red_b.at[pair], red_b.at[pair], ds_sem.at[k], dr_sem.at[k], pair=pair_peer(k))
        for k in range(1, npair)
    ]
    for c in sends_b:
        c.start()
    for k in range(1, npair):
        src = lax.rem(pair + npair - k, npair)
        remote(red_b.at[src], red_b.at[src], ds_sem.at[k], dr_sem.at[k], pair=pair_peer(k)).wait_recv()
    total = red_b[0]
    for k in range(1, npair):
        total = total + red_b[k]
    dots_ref[...] = total[0:2, :rhs] * (1.0 / nblk_total)
    for c in sends + sends_b:
        c.wait_send()

    @pl.when(has_right)
    def _():
        for ci in range(n // CC):
            give_back(ci).wait_send()

    @pl.when(has_left)
    def _():
        for ci in range(n // CC):
            for c in halo(ci):
                c.wait_send()


def on_device(points, inv_scales, direction, residual, skeleton):
    feats, n = points.shape
    rhs = direction.shape[0]
    nskel = skeleton.shape[1]
    nleaf = lax.axis_size("leaf")
    npair = lax.axis_size("pair")
    vmem = pl.BlockSpec(memory_space=pltpu.VMEM)
    dma = pltpu.SemaphoreType.DMA
    return pl.pallas_call(
        functools.partial(kernel, nleaf, npair, n * nleaf * npair),
        out_shape=(jax.ShapeDtypeStruct((rhs, n), f32), jax.ShapeDtypeStruct((2, rhs), f32)),
        in_specs=[vmem] * 5,
        out_specs=(vmem, vmem),
        scratch_shapes=[
            pltpu.VMEM((feats, n), f32),
            pltpu.VMEM((rhs, n), f32),
            pltpu.VMEM((rhs, n), f32),
            pltpu.VMEM((rhs, n), f32),
            pltpu.VMEM((4 * feats, n), bf16),
            pltpu.VMEM((8, n), f32),
            pltpu.VMEM((n, 4 * feats), bf16),
            pltpu.VMEM((n, 128), f32),
            pltpu.VMEM((2 * rhs, n), bf16),
            pltpu.VMEM((rhs, n), f32),
            pltpu.VMEM((nskel, n), f32),
            pltpu.VMEM((npair, nleaf * nskel, 128), f32),
            pltpu.VMEM((nleaf, 8, 128), f32),
            pltpu.VMEM((npair, 8, 128), f32),
            pltpu.VMEM((nskel, 128), f32),
            dma((2, n // CC)), dma((2, n // CC)),
            dma((n // CC,)), dma((n // CC,)),
            dma((nleaf,)), dma((nleaf,)),
            dma((npair,)), dma((npair,)),
            dma((nleaf,)), dma((nleaf,)),
            dma((npair,)), dma((npair,)),
        ],
        compiler_params=pltpu.CompilerParams(collective_id=0, has_side_effects=True, vmem_limit_bytes=60 * 1024 * 1024),
        name="matern_step",
    )(points, inv_scales.reshape(1, feats), direction, residual, skeleton)


def solution(mesh):
    return jax.shard_map(
        on_device,
        mesh=mesh,
        in_specs=(
            P(None, ("pair", "leaf")),
            P(),
            P(None, ("pair", "leaf")),
            P(None, ("pair", "leaf")),
            P(("pair", "leaf"), None),
        ),
        out_specs=(P(None, ("pair", "leaf")), P()),
        check_vma=False,
    )
```

```python
import functools
import math

import jax
import jax.numpy as jnp
from jax import lax
from jax.experimental import pallas as pl
from jax.experimental.pallas import tpu as pltpu
from jax.sharding import PartitionSpec as P

root_three = math.sqrt(3.0)
neg_log2e = -1.4426950408889634
nugget = 0.5
far_weight = 0.125
tiny = 1e-30
f32 = jnp.float32
bf16 = jnp.bfloat16
TI = 256
CC = 512
FIRST = 2
CH = 256


def matern_of(u):
    u = jnp.maximum(u, tiny)
    t = u * lax.rsqrt(u)
    return (1.0 + t) * jnp.exp2(t * neg_log2e)


def bdot(a, b):
    return jnp.dot(a, b, preferred_element_type=f32)


def bdot_nt(a, b):
    return lax.dot_general(a, b, (((1,), (1,)), ((), ())), preferred_element_type=f32)


def split(x):
    h = x.astype(bf16)
    return h, (x - h.astype(f32)).astype(bf16)


def kernel(
    nleaf, npair, nblk_total,
    pts_ref, inv_ref, dir_ref, res_ref, skel_ref,
    prod_ref, dots_ref,
    halo_p, halo_d, ret_out, ret_in, b_ref, nb_ref, st_ref, ns_ref, dd_ref, acc_ref, pacc_ref, ks_ref, ag_ref, red_a, red_b, tmp_ref,
    hs_sem, hr_sem, es_sem, er_sem, as_sem, ar_sem, bs_sem, br_sem, cs_sem, cr_sem, ds_sem, dr_sem,
):
    feats, n = pts_ref.shape
    rhs = dir_ref.shape[0]
    nskel = skel_ref.shape[1]
    leaf = lax.axis_index("leaf")
    pair = lax.axis_index("pair")

    def remote(src, dst, ss, rs, **dev):
        return pltpu.make_async_remote_copy(
            src_ref=src, dst_ref=dst, send_sem=ss, recv_sem=rs, device_id=dev,
            device_id_type=pl.DeviceIdType.MESH)

    def leaf_peer(k):
        return lax.rem(leaf + k, nleaf)

    def pair_peer(k):
        return lax.rem(pair + k, npair)

    barrier = pltpu.get_barrier_semaphore()
    for k in range(1, nleaf):
        pl.semaphore_signal(barrier, inc=1, device_id={"leaf": leaf_peer(k)}, device_id_type=pl.DeviceIdType.MESH)
    for k in range(1, npair):
        pl.semaphore_signal(barrier, inc=1, device_id={"pair": pair_peer(k)}, device_id_type=pl.DeviceIdType.MESH)
    pl.semaphore_wait(barrier, nleaf - 1 + npair - 1)

    has_left = leaf > 0
    has_right = leaf < nleaf - 1
    left = leaf_peer(nleaf - 1)
    right = leaf_peer(1)

    def chunk(ci):
        return pl.ds(pl.multiple_of(ci * CC, CC), CC)

    def halo(ci):
        cols = chunk(ci)
        return (
            remote(pts_ref.at[:, cols], halo_p.at[:, cols], hs_sem.at[0, ci], hr_sem.at[0, ci], leaf=left),
            remote(dir_ref.at[:, cols], halo_d.at[:, cols], hs_sem.at[1, ci], hr_sem.at[1, ci], leaf=left),
        )

    def give_back(ci):
        cols = chunk(ci)
        return remote(ret_out.at[:, cols], ret_in.at[:, cols], es_sem.at[ci], er_sem.at[ci], leaf=right)

    def send_halo(lo, hi):
        @pl.when(has_left)
        def _():
            for ci in range(lo, hi):
                for c in halo(ci):
                    c.start()

    send_halo(0, FIRST)

    eye = lax.broadcasted_iota(jnp.int32, (feats, feats), 0) == lax.broadcasted_iota(jnp.int32, (feats, feats), 1)
    inv_col = jnp.sum(jnp.where(eye, jnp.broadcast_to(inv_ref[...], (feats, feats)), 0.0), axis=1, keepdims=True) * root_three

    def halves(p_src, d_src, cols):
        p = p_src[:, cols] * inv_col
        h, l = split(p)
        hf, lf = h.astype(f32), l.astype(f32)
        q = hf + lf
        norm = jnp.sum(q * q, axis=0, keepdims=True)
        dh, dl = split(d_src[:, cols])
        return jnp.concatenate([h, l, h, l], axis=0), jnp.concatenate([dh, dl], axis=0), hf, lf, norm

    @pl.loop(0, n // CH)
    def _(ci):
        cols = pl.ds(pl.multiple_of(ci * CH, CH), CH)
        b, dd, hf, lf, norm = halves(pts_ref, dir_ref, cols)
        b_ref[:, cols] = b
        dd_ref[:, cols] = dd
        nb_ref[:, cols] = jnp.broadcast_to(norm, (8, CH))
        h2, l2 = hf * -2.0, lf * -2.0
        st_ref[cols, :] = jnp.concatenate([h2, h2, l2, l2], axis=0).T.astype(bf16)
        ns_ref[cols, :] = jnp.broadcast_to(norm, (128, CH)).T
        acc_ref[:, cols] = jnp.zeros((rhs, CH), f32)
        pacc_ref[:, cols] = jnp.zeros((rhs, CH), f32)

    nt = n // TI

    def tiles(rows_of, count, b, nb):
        nxt = bdot(st_ref[rows_of(0), :], b)
        for i in range(count):
            cross = nxt
            if i + 1 < count:
                nxt = bdot(st_ref[rows_of(i + 1), :], b)
            u = cross + jnp.concatenate([ns_ref[rows_of(i), :]] * (b.shape[1] // 128), axis=1) + nb
            now = (i,) + split(matern_of(u))
            if i:
                yield held
            held = now
        yield held

    def own_block():
        @pl.loop(0, nt)
        def _(jt):
            cols = pl.ds(pl.multiple_of(jt * TI, TI), TI)
            b = b_ref[:, cols]
            nb = nb_ref[0:1, cols]
            ddj = dd_ref[:, cols]
            a1 = jnp.zeros((2 * rhs, TI), f32)
            a2 = jnp.zeros((rhs, TI), f32)

            def rows_of(d):
                return pl.ds(pl.multiple_of(lax.rem(jt + nt - d, nt) * TI, TI), TI)

            later = []
            for d, kh, kl in tiles(rows_of, nt // 2 + 1, b, nb):
                rows = rows_of(d)
                a1 = a1 + bdot(dd_ref[:, rows], kh)
                a2 = a2 + bdot(dd_ref[:rhs, rows], kl)
                if 0 < d and 2 * d < nt:
                    r1 = bdot_nt(ddj, kh)
                    later.append((rows, r1[:rhs] + r1[rhs:] + bdot_nt(ddj[:rhs], kl)))
            acc_ref[:, cols] += a1[:rhs] + a1[rhs:] + a2
            for rows, part in later:
                acc_ref[:, rows] += part

    def pair_chunk(ci):
        for c in halo(ci):
            c.wait_recv()

        @pl.loop(0, CC // TI)
        def _(half):
            cols = pl.ds(pl.multiple_of(ci * CC + half * TI, TI), TI)
            b, ddj, _, _, nb = halves(halo_p, halo_d, cols)
            a1 = jnp.zeros((2 * rhs, TI), f32)
            a2 = jnp.zeros((rhs, TI), f32)
            for it, kh, kl in tiles(lambda i: slice(i * TI, (i + 1) * TI), nt, b, nb):
                rows = slice(it * TI, (it + 1) * TI)
                a1 = a1 + bdot(dd_ref[:, rows], kh)
                a2 = a2 + bdot(dd_ref[:rhs, rows], kl)
                r1 = bdot_nt(ddj, kh)
                pacc_ref[:, rows] += r1[:rhs] + r1[rhs:] + bdot_nt(ddj[:rhs], kl)
            ret_out[:, cols] = a1[:rhs] + a1[rhs:] + a2

        give_back(ci).start()

    onehot = (lax.broadcasted_iota(jnp.int32, (n, nskel), 0) == jnp.broadcast_to(skel_ref[...], (n, nskel)))
    onehot = jnp.where(onehot, 1.0, 0.0).astype(bf16)
    picked = bdot(b_ref[: 2 * feats, :], onehot)
    skel_rows = (picked[:feats] + picked[feats:]).T
    norm_s = jnp.sum(skel_rows * skel_rows, axis=1, keepdims=True)
    sh, sl = split(skel_rows)
    sh, sl = sh.astype(f32) * -2.0, sl.astype(f32) * -2.0
    cross_s = bdot(jnp.concatenate([sh, sh, sl, sl], axis=1).astype(bf16), b_ref[...])
    ksh, ksl = split(matern_of(norm_s + nb_ref[0:1, :] + cross_s))
    ks_ref[...] = jnp.concatenate([ksh, ksl], axis=0)
    part = bdot_nt(ks_ref[...], dd_ref[...])
    coeff_t = part[:nskel, :rhs] + part[:nskel, rhs:] + part[nskel:, :rhs] + part[nskel:, rhs:]
    pad = jnp.zeros((nskel, 128 - feats - rhs), f32)
    pack = jnp.concatenate([skel_rows, coeff_t, pad], axis=1)
    my_rows = pl.ds(pl.multiple_of(leaf * nskel, 8), nskel)
    ag_ref[pair, my_rows, :] = pack
    tmp_ref[...] = jnp.concatenate([skel_rows, jnp.zeros((nskel, 128 - feats), f32)], axis=1)

    stage_a = [
        remote(ag_ref.at[pair, my_rows, :], ag_ref.at[pair, my_rows, :], as_sem.at[k], ar_sem.at[k], leaf=leaf_peer(k))
        for k in range(1, nleaf)
    ]
    for c in stage_a:
        c.start()

    send_halo(FIRST, n // CC)
    own_block()

    stage_b = [
        remote(ag_ref.at[pair], ag_ref.at[pair], bs_sem.at[k], br_sem.at[k], pair=pair_peer(k))
        for k in range(1, npair)
    ]

    @pl.loop(0, n // CC)
    def _(ci):
        @pl.when(ci == n // CC - 1)
        def _():
            for k, c in enumerate(stage_a, 1):
                src_rows = pl.ds(pl.multiple_of(lax.rem(leaf + nleaf - k, nleaf) * nskel, 8), nskel)
                remote(ag_ref.at[pair, src_rows, :], ag_ref.at[pair, src_rows, :], as_sem.at[k], ar_sem.at[k], leaf=leaf_peer(k)).wait_recv()
            for c in stage_a:
                c.wait_send()
            for c in stage_b:
                c.start()

        @pl.when(has_right)
        def _():
            pair_chunk(ci)

    for k, c in enumerate(stage_b, 1):
        src = lax.rem(pair + npair - k, npair)
        remote(ag_ref.at[src], ag_ref.at[src], bs_sem.at[k], br_sem.at[k], pair=pair_peer(k)).wait_recv()
    for c in stage_b:
        c.wait_send()

    width = nleaf * nskel
    own_rows = tmp_ref[...]
    own_norm = jnp.sum(own_rows * own_rows, axis=1, keepdims=True)
    own_both = jnp.concatenate(split(own_rows), axis=0)
    is_pt = jnp.where(lax.broadcasted_iota(jnp.int32, (8, 128), 1) < feats, 1.0, 0.0).astype(bf16)
    column_leaf = lax.div(lax.broadcasted_iota(jnp.int32, (nskel, width), 1), nskel)
    near_mask = jnp.abs(column_leaf - leaf) <= 1
    q_t = jnp.zeros((nskel, 128), f32)
    for p in range(npair):
        ah, al = split(ag_ref[p])
        ar = ah.astype(f32) + al.astype(f32)
        sq = ar * ar
        s0, r1 = sq.astype(bf16), sq - sq.astype(bf16).astype(f32)
        s1, s2 = split(r1)
        norm_all = (bdot_nt(is_pt, s0) + bdot_nt(is_pt, s1) + bdot_nt(is_pt, s2))[0:1, :]
        cross = bdot_nt(own_both, ah) + bdot_nt(own_both, al)
        w = matern_of(own_norm + norm_all - 2.0 * (cross[:nskel] + cross[nskel:]))
        same = jnp.full((nskel, width), pair, jnp.int32) == p
        w = jnp.where(jnp.logical_and(same, near_mask), 0.0, w)
        wh, wl = split(w)
        part = bdot(jnp.concatenate([wh, wl], axis=0), ah)
        q_t = q_t + part[:nskel] + part[nskel:] + bdot(wh, al)
    q_t = q_t[:, feats : feats + rhs]
    qh, ql = split(q_t.T)
    far = bdot(jnp.concatenate([qh, ql], axis=0), ks_ref[:nskel, :])
    far = far[:rhs] + far[rhs:] + bdot(qh, ks_ref[nskel:, :])
    amplitude = 1.0 / math.sqrt(3.0 * n)
    direction = dir_ref[...]
    pair_part = amplitude * pacc_ref[...]
    product = nugget * direction + amplitude * (acc_ref[...] + far_weight * far) + pair_part
    prod_ref[...] = product
    residual = res_ref[...]
    squares = jnp.sum(residual * residual, axis=1, keepdims=True)
    curvature = jnp.sum(direction * (product + pair_part), axis=1, keepdims=True)
    lane = lax.broadcasted_iota(jnp.int32, (rhs, 128), 1)
    both = jnp.where(lane == 0, squares, jnp.where(lane == 1, curvature, 0.0))
    both = jnp.concatenate([both, jnp.zeros((128 - rhs, 128), f32)], axis=0).T[0:8, :]
    red_a[leaf] = both
    sends = [
        remote(red_a.at[leaf], red_a.at[leaf], cs_sem.at[k], cr_sem.at[k], leaf=leaf_peer(k))
        for k in range(1, nleaf)
    ]
    for c in sends:
        c.start()
    for k in range(1, nleaf):
        src = lax.rem(leaf + nleaf - k, nleaf)
        remote(red_a.at[src], red_a.at[src], cs_sem.at[k], cr_sem.at[k], leaf=leaf_peer(k)).wait_recv()
    total = red_a[0]
    for k in range(1, nleaf):
        total = total + red_a[k]
    red_b[pair] = total
    sends_b = [
        remote(red_b.at[pair], red_b.at[pair], ds_sem.at[k], dr_sem.at[k], pair=pair_peer(k))
        for k in range(1, npair)
    ]
    for c in sends_b:
        c.start()
    for k in range(1, npair):
        src = lax.rem(pair + npair - k, npair)
        remote(red_b.at[src], red_b.at[src], ds_sem.at[k], dr_sem.at[k], pair=pair_peer(k)).wait_recv()
    total = red_b[0]
    for k in range(1, npair):
        total = total + red_b[k]

    @pl.when(has_left)
    def _():
        for ci in range(n // CC):
            give_back(ci).wait_recv()
        prod_ref[...] += amplitude * ret_in[...]

    dots_ref[...] = total[0:2, :rhs] * (1.0 / nblk_total)
    for c in sends + sends_b:
        c.wait_send()

    @pl.when(has_right)
    def _():
        for ci in range(n // CC):
            give_back(ci).wait_send()

    @pl.when(has_left)
    def _():
        for ci in range(n // CC):
            for c in halo(ci):
                c.wait_send()


def on_device(points, inv_scales, direction, residual, skeleton):
    feats, n = points.shape
    rhs = direction.shape[0]
    nskel = skeleton.shape[1]
    nleaf = lax.axis_size("leaf")
    npair = lax.axis_size("pair")
    vmem = pl.BlockSpec(memory_space=pltpu.VMEM)
    dma = pltpu.SemaphoreType.DMA
    return pl.pallas_call(
        functools.partial(kernel, nleaf, npair, n * nleaf * npair),
        out_shape=(jax.ShapeDtypeStruct((rhs, n), f32), jax.ShapeDtypeStruct((2, rhs), f32)),
        in_specs=[vmem] * 5,
        out_specs=(vmem, vmem),
        scratch_shapes=[
            pltpu.VMEM((feats, n), f32),
            pltpu.VMEM((rhs, n), f32),
            pltpu.VMEM((rhs, n), f32),
            pltpu.VMEM((rhs, n), f32),
            pltpu.VMEM((4 * feats, n), bf16),
            pltpu.VMEM((8, n), f32),
            pltpu.VMEM((n, 4 * feats), bf16),
            pltpu.VMEM((n, 128), f32),
            pltpu.VMEM((2 * rhs, n), bf16),
            pltpu.VMEM((rhs, n), f32),
            pltpu.VMEM((rhs, n), f32),
            pltpu.VMEM((2 * nskel, n), bf16),
            pltpu.VMEM((npair, nleaf * nskel, 128), f32),
            pltpu.VMEM((nleaf, 8, 128), f32),
            pltpu.VMEM((npair, 8, 128), f32),
            pltpu.VMEM((nskel, 128), f32),
            dma((2, n // CC)), dma((2, n // CC)),
            dma((n // CC,)), dma((n // CC,)),
            dma((nleaf,)), dma((nleaf,)),
            dma((npair,)), dma((npair,)),
            dma((nleaf,)), dma((nleaf,)),
            dma((npair,)), dma((npair,)),
        ],
        compiler_params=pltpu.CompilerParams(collective_id=0, has_side_effects=True, vmem_limit_bytes=60 * 1024 * 1024),
        name="matern_step",
    )(points, inv_scales.reshape(1, feats), direction, residual, skeleton)


def solution(mesh):
    return jax.shard_map(
        on_device,
        mesh=mesh,
        in_specs=(
            P(None, ("pair", "leaf")),
            P(),
            P(None, ("pair", "leaf")),
            P(None, ("pair", "leaf")),
            P(("pair", "leaf"), None),
        ),
        out_specs=(P(None, ("pair", "leaf")), P()),
        check_vma=False,
    )
```

```python
import functools
import math

import jax
import jax.numpy as jnp
from jax import lax
from jax.experimental import pallas as pl
from jax.experimental.pallas import tpu as pltpu
from jax.sharding import PartitionSpec as P

root_three = math.sqrt(3.0)
neg_log2e = -1.4426950408889634
nugget = 0.5
far_weight = 0.125
tiny = 1e-30
f32 = jnp.float32
bf16 = jnp.bfloat16
TI = 256
CC = 512
FIRST = 2
CH = 256


def matern_of(u):
    u = jnp.maximum(u, tiny)
    t = u * lax.rsqrt(u)
    return (1.0 + t) * jnp.exp2(t * neg_log2e)


def bdot(a, b):
    return jnp.dot(a, b, preferred_element_type=f32)


def bdot_nt(a, b):
    return lax.dot_general(a, b, (((1,), (1,)), ((), ())), preferred_element_type=f32)


def split(x):
    h = x.astype(bf16)
    return h, (x - h.astype(f32)).astype(bf16)


def kernel(
    nleaf, npair, nblk_total,
    pts_ref, inv_ref, dir_ref, res_ref, skel_ref,
    prod_ref, dots_ref,
    halo_p, halo_d, ret_out, ret_in, b_ref, nb_ref, st_ref, ns_ref, dd_ref, acc_ref, pacc_ref, ks_ref, ag_ref, red_a, red_b, tmp_ref,
    hs_sem, hr_sem, es_sem, er_sem, as_sem, ar_sem, bs_sem, br_sem, cs_sem, cr_sem, ds_sem, dr_sem,
):
    feats, n = pts_ref.shape
    rhs = dir_ref.shape[0]
    nskel = skel_ref.shape[1]
    leaf = lax.axis_index("leaf")
    pair = lax.axis_index("pair")

    def remote(src, dst, ss, rs, **dev):
        return pltpu.make_async_remote_copy(
            src_ref=src, dst_ref=dst, send_sem=ss, recv_sem=rs, device_id=dev,
            device_id_type=pl.DeviceIdType.MESH)

    def leaf_peer(k):
        return lax.rem(leaf + k, nleaf)

    def pair_peer(k):
        return lax.rem(pair + k, npair)

    barrier = pltpu.get_barrier_semaphore()
    for k in range(1, nleaf):
        pl.semaphore_signal(barrier, inc=1, device_id={"leaf": leaf_peer(k)}, device_id_type=pl.DeviceIdType.MESH)
    for k in range(1, npair):
        pl.semaphore_signal(barrier, inc=1, device_id={"pair": pair_peer(k)}, device_id_type=pl.DeviceIdType.MESH)
    pl.semaphore_wait(barrier, nleaf - 1 + npair - 1)

    has_left = leaf > 0
    has_right = leaf < nleaf - 1
    left = leaf_peer(nleaf - 1)
    right = leaf_peer(1)

    def chunk(ci):
        return pl.ds(pl.multiple_of(ci * CC, CC), CC)

    def halo(ci):
        cols = chunk(ci)
        return (
            remote(pts_ref.at[:, cols], halo_p.at[:, cols], hs_sem.at[0, ci], hr_sem.at[0, ci], leaf=left),
            remote(dir_ref.at[:, cols], halo_d.at[:, cols], hs_sem.at[1, ci], hr_sem.at[1, ci], leaf=left),
        )

    def give_back(ci):
        cols = chunk(ci)
        return remote(ret_out.at[:, cols], ret_in.at[:, cols], es_sem.at[ci], er_sem.at[ci], leaf=right)

    def send_halo(lo, hi):
        @pl.when(has_left)
        def _():
            for ci in range(lo, hi):
                for c in halo(ci):
                    c.start()

    send_halo(0, FIRST)

    eye = lax.broadcasted_iota(jnp.int32, (feats, feats), 0) == lax.broadcasted_iota(jnp.int32, (feats, feats), 1)
    inv_col = jnp.sum(jnp.where(eye, jnp.broadcast_to(inv_ref[...], (feats, feats)), 0.0), axis=1, keepdims=True) * root_three

    def halves(p_src, d_src, cols):
        p = p_src[:, cols] * inv_col
        h, l = split(p)
        hf, lf = h.astype(f32), l.astype(f32)
        q = hf + lf
        norm = jnp.sum(q * q, axis=0, keepdims=True)
        dh, dl = split(d_src[:, cols])
        return jnp.concatenate([h, l, h, l], axis=0), jnp.concatenate([dh, dl], axis=0), hf, lf, norm

    @pl.loop(0, n // CH)
    def _(ci):
        cols = pl.ds(pl.multiple_of(ci * CH, CH), CH)
        b, dd, hf, lf, norm = halves(pts_ref, dir_ref, cols)
        b_ref[:, cols] = b
        dd_ref[:, cols] = dd
        nb_ref[:, cols] = jnp.broadcast_to(norm, (8, CH))
        h2, l2 = hf * -2.0, lf * -2.0
        st_ref[cols, :] = jnp.concatenate([h2, h2, l2, l2], axis=0).T.astype(bf16)
        ns_ref[cols, :] = jnp.broadcast_to(norm, (128, CH)).T
        acc_ref[:, cols] = jnp.zeros((rhs, CH), f32)
        pacc_ref[:, cols] = jnp.zeros((rhs, CH), f32)

    nt = n // TI

    def tiles(rows_of, count, b, nb):
        nxt = bdot(st_ref[rows_of(0), :], b)
        for i in range(count):
            cross = nxt
            if i + 1 < count:
                nxt = bdot(st_ref[rows_of(i + 1), :], b)
            u = cross + jnp.concatenate([ns_ref[rows_of(i), :]] * (b.shape[1] // 128), axis=1) + nb
            now = (i,) + split(matern_of(u))
            if i:
                yield held
            held = now
        yield held

    def own_block():
        @pl.loop(0, nt)
        def _(jt):
            cols = pl.ds(pl.multiple_of(jt * TI, TI), TI)
            b = b_ref[:, cols]
            nb = nb_ref[0:1, cols]
            ddj = dd_ref[:, cols]
            a1 = jnp.zeros((2 * rhs, TI), f32)
            a2 = jnp.zeros((rhs, TI), f32)

            def rows_of(d):
                return pl.ds(pl.multiple_of(lax.rem(jt + nt - d, nt) * TI, TI), TI)

            later = []
            for d, kh, kl in tiles(rows_of, nt // 2 + 1, b, nb):
                rows = rows_of(d)
                a1 = a1 + bdot(dd_ref[:, rows], kh)
                a2 = a2 + bdot(dd_ref[:rhs, rows], kl)
                if 0 < d and 2 * d < nt:
                    r1 = bdot_nt(ddj, kh)
                    later.append((rows, r1[:rhs] + r1[rhs:] + bdot_nt(ddj[:rhs], kl)))
            acc_ref[:, cols] += a1[:rhs] + a1[rhs:] + a2
            for rows, part in later:
                acc_ref[:, rows] += part

    def pair_chunk(ci):
        for c in halo(ci):
            c.wait_recv()

        @pl.loop(0, CC // TI)
        def _(half):
            cols = pl.ds(pl.multiple_of(ci * CC + half * TI, TI), TI)
            b, ddj, _, _, nb = halves(halo_p, halo_d, cols)
            a1 = jnp.zeros((2 * rhs, TI), f32)
            a2 = jnp.zeros((rhs, TI), f32)
            for it, kh, kl in tiles(lambda i: slice(i * TI, (i + 1) * TI), nt, b, nb):
                rows = slice(it * TI, (it + 1) * TI)
                a1 = a1 + bdot(dd_ref[:, rows], kh)
                a2 = a2 + bdot(dd_ref[:rhs, rows], kl)
                r1 = bdot_nt(ddj, kh)
                pacc_ref[:, rows] += r1[:rhs] + r1[rhs:] + bdot_nt(ddj[:rhs], kl)
            ret_out[:, cols] = a1[:rhs] + a1[rhs:] + a2

        give_back(ci).start()

    onehot = (lax.broadcasted_iota(jnp.int32, (n, nskel), 0) == jnp.broadcast_to(skel_ref[...], (n, nskel)))
    onehot = jnp.where(onehot, 1.0, 0.0).astype(bf16)
    picked = bdot(b_ref[: 2 * feats, :], onehot)
    skel_rows = (picked[:feats] + picked[feats:]).T
    norm_s = jnp.sum(skel_rows * skel_rows, axis=1, keepdims=True)
    sh, sl = split(skel_rows)
    sh, sl = sh.astype(f32) * -2.0, sl.astype(f32) * -2.0
    cross_s = bdot(jnp.concatenate([sh, sh, sl, sl], axis=1).astype(bf16), b_ref[...])
    ksh, ksl = split(matern_of(norm_s + nb_ref[0:1, :] + cross_s))
    ks_ref[...] = jnp.concatenate([ksh, ksl], axis=0)
    part = bdot_nt(ks_ref[...], dd_ref[...])
    coeff_t = part[:nskel, :rhs] + part[:nskel, rhs:] + part[nskel:, :rhs] + part[nskel:, rhs:]
    pad = jnp.zeros((nskel, 128 - feats - rhs), f32)
    pack = jnp.concatenate([skel_rows, coeff_t, pad], axis=1)
    my_rows = pl.ds(pl.multiple_of(leaf * nskel, 8), nskel)
    ag_ref[pair, my_rows, :] = pack
    tmp_ref[...] = jnp.concatenate([skel_rows, jnp.zeros((nskel, 128 - feats), f32)], axis=1)

    stage_a = [
        remote(ag_ref.at[pair, my_rows, :], ag_ref.at[pair, my_rows, :], as_sem.at[k], ar_sem.at[k], leaf=leaf_peer(k))
        for k in range(1, nleaf)
    ]
    for c in stage_a:
        c.start()

    send_halo(FIRST, n // CC)
    own_block()

    stage_b = [
        remote(ag_ref.at[pair], ag_ref.at[pair], bs_sem.at[k], br_sem.at[k], pair=pair_peer(k))
        for k in range(1, npair)
    ]

    @pl.loop(0, n // CC)
    def _(ci):
        @pl.when(ci == 1)
        def _():
            for k, c in enumerate(stage_a, 1):
                src_rows = pl.ds(pl.multiple_of(lax.rem(leaf + nleaf - k, nleaf) * nskel, 8), nskel)
                remote(ag_ref.at[pair, src_rows, :], ag_ref.at[pair, src_rows, :], as_sem.at[k], ar_sem.at[k], leaf=leaf_peer(k)).wait_recv()
            for c in stage_a:
                c.wait_send()
            for c in stage_b:
                c.start()

        @pl.when(has_right)
        def _():
            pair_chunk(ci)

    for k, c in enumerate(stage_b, 1):
        src = lax.rem(pair + npair - k, npair)
        remote(ag_ref.at[src], ag_ref.at[src], bs_sem.at[k], br_sem.at[k], pair=pair_peer(k)).wait_recv()
    for c in stage_b:
        c.wait_send()

    width = nleaf * nskel
    own_rows = tmp_ref[...]
    own_norm = jnp.sum(own_rows * own_rows, axis=1, keepdims=True)
    own_both = jnp.concatenate(split(own_rows), axis=0)
    is_pt = jnp.where(lax.broadcasted_iota(jnp.int32, (8, 128), 1) < feats, 1.0, 0.0).astype(bf16)
    column_leaf = lax.div(lax.broadcasted_iota(jnp.int32, (nskel, width), 1), nskel)
    near_mask = jnp.abs(column_leaf - leaf) <= 1
    q_t = jnp.zeros((nskel, 128), f32)
    for p in range(npair):
        ah, al = split(ag_ref[p])
        ar = ah.astype(f32) + al.astype(f32)
        sq = ar * ar
        s0, r1 = sq.astype(bf16), sq - sq.astype(bf16).astype(f32)
        s1, s2 = split(r1)
        norm_all = (bdot_nt(is_pt, s0) + bdot_nt(is_pt, s1) + bdot_nt(is_pt, s2))[0:1, :]
        cross = bdot_nt(own_both, ah) + bdot_nt(own_both, al)
        w = matern_of(own_norm + norm_all - 2.0 * (cross[:nskel] + cross[nskel:]))
        same = jnp.full((nskel, width), pair, jnp.int32) == p
        w = jnp.where(jnp.logical_and(same, near_mask), 0.0, w)
        wh, wl = split(w)
        part = bdot(jnp.concatenate([wh, wl], axis=0), ah)
        q_t = q_t + part[:nskel] + part[nskel:] + bdot(wh, al)
    q_t = q_t[:, feats : feats + rhs]
    qh, ql = split(q_t.T)
    far = bdot(jnp.concatenate([qh, ql], axis=0), ks_ref[:nskel, :])
    far = far[:rhs] + far[rhs:] + bdot(qh, ks_ref[nskel:, :])
    amplitude = 1.0 / math.sqrt(3.0 * n)
    direction = dir_ref[...]
    pair_part = amplitude * pacc_ref[...]
    product = nugget * direction + amplitude * (acc_ref[...] + far_weight * far) + pair_part
    prod_ref[...] = product
    residual = res_ref[...]
    squares = jnp.sum(residual * residual, axis=1, keepdims=True)
    curvature = jnp.sum(direction * (product + pair_part), axis=1, keepdims=True)
    lane = lax.broadcasted_iota(jnp.int32, (rhs, 128), 1)
    both = jnp.where(lane == 0, squares, jnp.where(lane == 1, curvature, 0.0))
    both = jnp.concatenate([both, jnp.zeros((128 - rhs, 128), f32)], axis=0).T[0:8, :]
    red_a[leaf] = both
    sends = [
        remote(red_a.at[leaf], red_a.at[leaf], cs_sem.at[k], cr_sem.at[k], leaf=leaf_peer(k))
        for k in range(1, nleaf)
    ]
    for c in sends:
        c.start()
    for k in range(1, nleaf):
        src = lax.rem(leaf + nleaf - k, nleaf)
        remote(red_a.at[src], red_a.at[src], cs_sem.at[k], cr_sem.at[k], leaf=leaf_peer(k)).wait_recv()
    total = red_a[0]
    for k in range(1, nleaf):
        total = total + red_a[k]
    red_b[pair] = total
    sends_b = [
        remote(red_b.at[pair], red_b.at[pair], ds_sem.at[k], dr_sem.at[k], pair=pair_peer(k))
        for k in range(1, npair)
    ]
    for c in sends_b:
        c.start()
    for k in range(1, npair):
        src = lax.rem(pair + npair - k, npair)
        remote(red_b.at[src], red_b.at[src], ds_sem.at[k], dr_sem.at[k], pair=pair_peer(k)).wait_recv()
    total = red_b[0]
    for k in range(1, npair):
        total = total + red_b[k]

    @pl.when(has_left)
    def _():
        for ci in range(n // CC):
            give_back(ci).wait_recv()
        prod_ref[...] += amplitude * ret_in[...]

    dots_ref[...] = total[0:2, :rhs] * (1.0 / nblk_total)
    for c in sends + sends_b:
        c.wait_send()

    @pl.when(has_right)
    def _():
        for ci in range(n // CC):
            give_back(ci).wait_send()

    @pl.when(has_left)
    def _():
        for ci in range(n // CC):
            for c in halo(ci):
                c.wait_send()


def on_device(points, inv_scales, direction, residual, skeleton):
    feats, n = points.shape
    rhs = direction.shape[0]
    nskel = skeleton.shape[1]
    nleaf = lax.axis_size("leaf")
    npair = lax.axis_size("pair")
    vmem = pl.BlockSpec(memory_space=pltpu.VMEM)
    dma = pltpu.SemaphoreType.DMA
    return pl.pallas_call(
        functools.partial(kernel, nleaf, npair, n * nleaf * npair),
        out_shape=(jax.ShapeDtypeStruct((rhs, n), f32), jax.ShapeDtypeStruct((2, rhs), f32)),
        in_specs=[vmem] * 5,
        out_specs=(vmem, vmem),
        scratch_shapes=[
            pltpu.VMEM((feats, n), f32),
            pltpu.VMEM((rhs, n), f32),
            pltpu.VMEM((rhs, n), f32),
            pltpu.VMEM((rhs, n), f32),
            pltpu.VMEM((4 * feats, n), bf16),
            pltpu.VMEM((8, n), f32),
            pltpu.VMEM((n, 4 * feats), bf16),
            pltpu.VMEM((n, 128), f32),
            pltpu.VMEM((2 * rhs, n), bf16),
            pltpu.VMEM((rhs, n), f32),
            pltpu.VMEM((rhs, n), f32),
            pltpu.VMEM((2 * nskel, n), bf16),
            pltpu.VMEM((npair, nleaf * nskel, 128), f32),
            pltpu.VMEM((nleaf, 8, 128), f32),
            pltpu.VMEM((npair, 8, 128), f32),
            pltpu.VMEM((nskel, 128), f32),
            dma((2, n // CC)), dma((2, n // CC)),
            dma((n // CC,)), dma((n // CC,)),
            dma((nleaf,)), dma((nleaf,)),
            dma((npair,)), dma((npair,)),
            dma((nleaf,)), dma((nleaf,)),
            dma((npair,)), dma((npair,)),
        ],
        compiler_params=pltpu.CompilerParams(collective_id=0, has_side_effects=True, vmem_limit_bytes=60 * 1024 * 1024),
        name="matern_step",
    )(points, inv_scales.reshape(1, feats), direction, residual, skeleton)


def solution(mesh):
    return jax.shard_map(
        on_device,
        mesh=mesh,
        in_specs=(
            P(None, ("pair", "leaf")),
            P(),
            P(None, ("pair", "leaf")),
            P(None, ("pair", "leaf")),
            P(("pair", "leaf"), None),
        ),
        out_specs=(P(None, ("pair", "leaf")), P()),
        check_vma=False,
    )
```
